256 devices in a mesh: samp: 4 (over y), snp: 64 (over x, z, core).
Axes of the slice: x: 4, y: 4, z: 8, core: 2. Of those that a mesh axis runs over, the one named last changes fastest.
Arguments:
- dosage: bfloat16 [8192, 32768], P('samp', 'snp'), may hold values from 0 to 2
- band_width: int32 [64], P('snp'), may hold values from 1 to 3, as said below
- marginal: float32 [32768, 64], P('snp'), may hold values from -6 to 6
- penalty: float32 [64], replicated, may hold values from 4 to 16
Outputs:
- effects: float32 [32768, 64], P('snp')
- residual: float32 [32768, 64], P('snp')
The draws below stay inside these ranges and needn't reach their ends.
Inputs may be any that keep to these rules, and one draw needn't show every extreme that they name: `band_width`: every draw has a block with 3 neighbours and one with a single neighbour.
All inputs are finite; a program needn't handle non-finite values.
Results may differ from the reference program's by a relative error of at most 0.00087.
Values may be sent and summed in bfloat16 or wider, within the bound.
A program may use at most 64 MiB of HBM per device.

```python
import math
import jax
import jax.numpy as jnp
from jax import lax

BLK = 512
WMAX = 3
TRAITS = 64
ITERS = 2
SAMPLES = 8192
NBLK = 64
SNPS = 32768


def draw_dosage(key, part):
    subkeys = jax.random.split(jax.random.fold_in(key, 11), 4)
    decay_rate = math.exp(-1.0 / 128.0)
    innovations = jax.random.normal(subkeys[0], (SNPS, SAMPLES), jnp.float32)

    def advance(carry, fresh):
        updated = decay_rate * carry + math.sqrt(1.0 - decay_rate * decay_rate) * fresh
        return (updated, updated)
    starting = jax.random.normal(subkeys[1], (SAMPLES,), jnp.float32)
    _, ancestry_walk = lax.scan(advance, starting, innovations)
    local_noise = jax.random.normal(subkeys[2], (SAMPLES, SNPS), jnp.float32)
    frequency = jax.random.uniform(subkeys[3], (SNPS,), jnp.float32, -1.2, 1.2)
    latent = 0.9 * ancestry_walk.T + 0.7 * local_noise + frequency
    return (2.0 * jax.nn.sigmoid(latent)).astype(jnp.bfloat16)


def draw_band_width(key, part):
    subkeys = jax.random.split(jax.random.fold_in(key, 23), 2)
    widths = jax.random.randint(subkeys[0], (NBLK,), 1, WMAX + 1)
    shuffled = jax.random.permutation(subkeys[1], NBLK)
    return widths.at[shuffled[0]].set(WMAX).at[shuffled[1]].set(1).astype(jnp.int32)


def shard_levels(rng, dims, shards, low, largest):
    level, own = 1.0, jax.random.fold_in(rng, 6)
    for position, shards_of in shards:
        draws = jnp.exp(jax.random.uniform(jax.random.fold_in(own, position), (shards_of,), jnp.float32, low / len(shards), largest / len(shards)))
        level = level * jnp.repeat(draws, dims[position] // shards_of).reshape([-1 if axis == position else 1 for axis in range(len(dims))])
    return level


def gaussian(stream_key, shape, width, limit, shards=(), kind=jnp.bfloat16):
    array = jax.random.normal(stream_key, shape, jnp.float32) * width
    if len(shards) > 0:
        array = shard_levels(stream_key, shape, shards, -0.22, 0.18) * array
    return jnp.clip(array, min=-limit, max=limit).astype(kind)


def setup_inputs(seed: int = 0) -> dict:
    key_list = jax.random.split(jax.random.key(seed), 5)
    dosage = draw_dosage(jax.random.fold_in(key_list[4], 71), 0)
    band_width = draw_band_width(jax.random.fold_in(key_list[4], 71), 0)
    marginal = gaussian(key_list[2], (SNPS, TRAITS), 1.0, 6.0, ((0, 64),), jnp.float32)
    penalty = jnp.clip(jnp.exp(jax.random.uniform(key_list[3], (TRAITS,), jnp.float32, math.log(4.0), math.log(16.0))), 4.0, 16.0)
    return dict(dosage=dosage, band_width=band_width, marginal=marginal, penalty=penalty)


def reference(dosage, band_width, marginal, penalty):
    samples = dosage.shape[0]
    genotype = dosage.astype(jnp.float32)
    center = lax.optimization_barrier(jnp.sum(genotype, 0)) / samples
    spread = lax.optimization_barrier(jnp.sum(genotype * genotype, 0)) / samples - center * center
    scaled = ((genotype - center) * lax.rsqrt(spread + 1e-05)).astype(jnp.bfloat16)
    padded = jnp.concatenate([scaled, jnp.zeros((samples, WMAX * BLK), jnp.bfloat16)], 1)
    offsets = jnp.arange((WMAX + 1) * BLK, dtype=jnp.int32) // BLK

    def band_rows(index):
        start = (index * BLK).astype(jnp.int32)
        own_cols = lax.dynamic_slice_in_dim(scaled, start, BLK, 1)
        wide_cols = lax.dynamic_slice_in_dim(padded, start, (WMAX + 1) * BLK, 1)
        gram = jnp.dot(own_cols.T, wide_cols, preferred_element_type=jnp.float32)
        return jnp.where(offsets[None, :] <= band_width[index], gram, 0.0) / samples
    ld_band = lax.map(band_rows, jnp.arange(NBLK, dtype=jnp.int32))
    highest = lax.Precision.HIGHEST

    def operate(direction):
        blocks = direction.reshape(NBLK, BLK, direction.shape[1])
        padded_dir = jnp.concatenate([blocks, jnp.zeros((WMAX, BLK, blocks.shape[2]), blocks.dtype)], 0)
        result = jnp.zeros_like(blocks)
        for offset in range(WMAX + 1):
            ld_block = ld_band[:, :, offset * BLK:(offset + 1) * BLK]
            result = result + jnp.einsum('iab,ibt->iat', ld_block, padded_dir[offset:offset + NBLK], precision=highest)
            if offset > 0:
                moved = jnp.einsum('iab,iat->ibt', ld_block, blocks, precision=highest)
                result = result.at[offset:].add(moved[:NBLK - offset])
        return result.reshape(direction.shape) + penalty * direction
    effects = jnp.zeros_like(marginal)
    residual = marginal
    direction = marginal
    norm_now = lax.optimization_barrier(jnp.sum(residual * residual, 0))
    for sweep in range(ITERS):
        imaged = operate(direction)
        step_size = norm_now / lax.optimization_barrier(jnp.sum(direction * imaged, 0))
        effects = effects + step_size * direction
        residual = residual - step_size * imaged
        norm_next = lax.optimization_barrier(jnp.sum(residual * residual, 0))
        direction = residual + norm_next / norm_now * direction
        norm_now = norm_next
    return (effects, residual)
```

```python
import functools

import jax
import jax.numpy as jnp
from jax import lax
from jax.experimental import pallas as pl
from jax.experimental.pallas import tpu as pltpu
from jax.sharding import PartitionSpec as P

MESH = pl.DeviceIdType.MESH
CHUNKS = 4
LINE = 16


def two_parts(x):
    high = x.astype(jnp.bfloat16)
    low = (x - high.astype(jnp.float32)).astype(jnp.bfloat16)
    return jnp.concatenate([high, low], 0)


def lanes_to_row(x):
    width = x.shape[1]
    total = x[:, 0:128]
    for start in range(128, width, 128):
        total = total + x[:, start : start + 128]
    return jnp.sum(total.T, axis=0, keepdims=True)


def kernel(
    n_samp, n_snp, line, samples,
    dosage, width, marginal, penalty,
    effects, residual,
    grid, marg, stats, widths, vec_t, own, own_f32, near, part, fold, fold_in,
    tile_a, tile_b, factors,
    load_sem, marg_sem, stat_send, stat_recv, width_send, width_recv,
    u_send, u_recv, fold_send, fold_recv, a_send, a_recv, b_send, b_recv,
):
    chunk = grid.shape[1]
    block = grid.shape[2]
    traits = vec_t.shape[0]
    half = traits // 2
    y = lax.axis_index("samp")
    i = lax.axis_index("snp")
    core = lax.rem(i, 2)
    side = 2 * core - 1

    def snp_at(step):
        return lax.rem(i + step + n_snp, n_snp)

    def samp_at(step):
        return lax.rem(y + step, n_samp)

    loads = []
    for k in range(CHUNKS):
        copy = pltpu.make_async_copy(
            dosage.at[pl.ds(k * chunk, chunk), :], grid.at[k], load_sem.at[k]
        )
        copy.start()
        loads.append(copy)
    marg_copy = pltpu.make_async_copy(marginal, marg, marg_sem)
    marg_copy.start()

    spot = lax.rem(i, line)
    base = i - spot
    line_peers = [(y, base + lax.rem(spot + d, line)) for d in range(1, line)]
    n_lines = n_snp // line
    plane_peers = []
    for dx in range(n_lines):
        for dy in range(n_samp):
            if dx or dy:
                plane_peers.append((samp_at(dy), lax.rem(i + line * dx, n_snp)))
    near_peers = [(y, snp_at(d)) for d in (-3, -2, -1, 1, 2, 3)]
    barrier = pltpu.get_barrier_semaphore()
    everyone = near_peers + line_peers + plane_peers
    for peer in everyone:
        pl.semaphore_signal(barrier, inc=1, device_id=peer, device_id_type=MESH)

    def send(src, dst, send_sem, recv_sem, peer):
        return pltpu.make_async_remote_copy(
            src_ref=src, dst_ref=dst, send_sem=send_sem, recv_sem=recv_sem,
            device_id=peer, device_id_type=MESH,
        )

    own_width = width[0].astype(jnp.float32)
    widths[0] = jnp.full(widths.shape[1:], own_width, jnp.float32)
    rows = 64
    sums = (jnp.zeros((8, block), jnp.float32), jnp.zeros((8, block), jnp.float32))
    for k in range(CHUNKS):
        loads[k].wait()

        def add_rows(r, carry, k=k):
            first, second = carry
            g = grid[k, pl.ds(pl.multiple_of(r * rows, rows), rows), :].astype(jnp.float32)
            g = g.reshape(rows // 8, 8, block)
            return first + jnp.sum(g, 0), second + jnp.sum(g * g, 0)

        sums = lax.fori_loop(0, chunk // rows, add_rows, sums)
    stats[0, 0:1, :] = jnp.sum(sums[0], 0, keepdims=True)
    stats[0, 1:2, :] = jnp.sum(sums[1], 0, keepdims=True)

    pl.semaphore_wait(barrier, len(everyone))

    started = []
    stat_copies = []
    for d in range(1, n_samp):
        copy = send(
            stats.at[0], stats.at[d], stat_send.at[d - 1], stat_recv.at[d - 1],
            (samp_at(d), i),
        )
        copy.start()
        stat_copies.append(copy)
    width_copies = []
    for d in (1, 2, 3):
        copy = send(
            widths.at[0], widths.at[d], width_send.at[d - 1], width_recv.at[d - 1],
            (y, snp_at(d)),
        )
        copy.start()
        width_copies.append(copy)

    marg_copy.wait()
    vec_t[...] = marg[...]
    m0 = lanes_to_row(marg[...] * marg[...])
    vector = two_parts(marg[...])

    for copy in stat_copies:
        copy.wait_recv()
    first = (stats[0] + stats[2]) + (stats[1] + stats[3])
    center = first[0:1, :] / samples
    spread = first[1:2, :] / samples - center * center
    scale = lax.rsqrt(spread + 1e-05)

    partner = (y, snp_at(-side))
    forth = (y, snp_at(2 * side))
    back = (y, snp_at(-2 * side))
    outer = (y, snp_at(side))

    masks = {}

    def make_masks():
        for copy in width_copies:
            copy.wait_recv()
        right = {}
        left = {}
        for d in (1, 2, 3):
            allowed = jnp.where(widths[0][0:1, 0:1] >= d, 1.0, 0.0)
            inside = jnp.where(i + d < n_snp, 1.0, 0.0)
            right[d] = allowed * inside
            allowed = jnp.where(widths[d][0:1, 0:1] >= d, 1.0, 0.0)
            inside = jnp.where(i - d >= 0, 1.0, 0.0)
            left[d] = allowed * inside
        turn = jnp.where(core == 1, 1.0, 0.0)
        for d in (1, 2, 3):
            masks["in", d] = turn * left[d] + (1.0 - turn) * right[d]
            masks["out", d] = turn * right[d] + (1.0 - turn) * left[d]

    order = ((0, ("in", 1)), (1, ("in", 2)), (2, ("in", 3)),
             (3, ("out", 1)), (4, ("out", 2)), (5, ("out", 3)))

    def fold_copy(p, leg, piece, peer):
        cut = pl.ds(piece * half, half)
        source = part.at[p] if leg == 0 else fold.at[p]
        return send(
            source.at[cut], fold_in.at[p, leg, cut],
            fold_send.at[p, leg, piece], fold_recv.at[p, leg, piece], peer,
        )

    flipped = y + 1 - 2 * lax.rem(y, 2)
    mirrored = n_samp - 1 - y
    images = []
    trail = None
    cross = []
    for p in range(2):
        moves = []
        for k in range(CHUNKS):
            if p == 0:
                def standardize(r, carry, k=k):
                    cut = pl.ds(pl.multiple_of(r * rows, rows), rows)
                    g = grid[k, cut, :].astype(jnp.float32)
                    grid[k, cut, :] = ((g - center) * scale).astype(jnp.bfloat16)
                    return carry

                lax.fori_loop(0, chunk // rows, standardize, 0)
            u = lax.dot_general(
                vector, grid[k], (((1,), (1,)), ((), ())),
                preferred_element_type=jnp.float32,
            )
            u = u[:traits] + u[traits:]
            own_f32[k] = u
            own[p, k] = u.astype(jnp.bfloat16)
            here = []
            for leg, (slot, peer) in enumerate(((1, forth), (4, back), (0, partner))):
                copy = send(
                    own.at[p, k], near.at[p, slot, k],
                    u_send.at[p, slot, k], u_recv.at[p, slot, k], peer,
                )
                copy.start()
                here.append(copy)
            moves.append(here)
        if p == 0:
            make_masks()
        passed = []
        for k in range(CHUNKS):
            inward, outward, beside = moves[k]
            inward.wait_recv()
            relay = send(
                near.at[p, 1, k], near.at[p, 5, k],
                u_send.at[p, 5, k], u_recv.at[p, 5, k], outer,
            )
            relay.start()
            to_one = send(
                near.at[p, 1, k], near.at[p, 3, k],
                u_send.at[p, 3, k], u_recv.at[p, 3, k], partner,
            )
            to_one.start()
            outward.wait_recv()
            to_three = send(
                near.at[p, 4, k], near.at[p, 2, k],
                u_send.at[p, 2, k], u_recv.at[p, 2, k], partner,
            )
            to_three.start()
            passed.append((to_one, to_three, relay))
        total = jnp.zeros((2 * traits, block), jnp.float32)
        for k in range(CHUNKS):
            moves[k][2].wait_recv()
            for copy in passed[k]:
                copy.wait_recv()
            u = own_f32[k]
            w = u
            for slot, key in order:
                w = w + masks[key] * near[p, slot, k].astype(jnp.float32)
            if p == 1:
                piece = u * w
                folded = piece[:, 0:128]
                for start in range(128, chunk, 128):
                    folded = folded + piece[:, start : start + 128]
                cross.append(folded)
            total = total + lax.dot_general(
                two_parts(w), grid[k], (((1,), (0,)), ((), ())),
                preferred_element_type=jnp.float32,
            )
        part[p] = (total[:traits] + total[traits:]) * (1.0 / samples)
        legs = [fold_copy(p, 0, 0, (flipped, i)), fold_copy(p, 0, 1, (mirrored, i))]
        for copy in legs:
            copy.start()
        if p == 1:
            m3 = lanes_to_row(cross[0] + cross[1] + cross[2] + cross[3]) * (1.0 / samples)
            tile_a[spot] = jnp.zeros(tile_a.shape[1:], jnp.float32)
            share = 1.0 / n_samp
            tile_a[spot, 0:1, 0:traits] = m0 * share
            tile_a[spot, 1:2, 0:traits] = m1 * share
            tile_a[spot, 2:3, 0:traits] = m2 * share
            tile_a[spot, 3:4, 0:traits] = m3
            line_copies = []
            for d, peer in enumerate(line_peers):
                copy = send(
                    tile_a.at[spot], tile_a.at[spot], a_send.at[d], a_recv.at[d], peer
                )
                copy.start()
                line_copies.append(copy)
        for copy in legs:
            copy.wait_recv()
        fold[p] = part[p] + fold_in[p, 0]
        legs_b = [fold_copy(p, 1, 0, (mirrored, i)), fold_copy(p, 1, 1, (flipped, i))]
        for copy in legs_b:
            copy.start()
        if p == 1:
            for copy in line_copies:
                copy.wait_recv()
            summed = tile_a[0]
            for q in range(1, line):
                summed = summed + tile_a[q]
            seat = (i // line) * n_samp + y
            tile_b[seat] = summed
            plane_copies = []
            for d, peer in enumerate(plane_peers):
                copy = send(
                    tile_b.at[seat], tile_b.at[seat], b_send.at[d], b_recv.at[d], peer
                )
                copy.start()
                plane_copies.append(copy)
        for copy in legs_b:
            copy.wait_recv()
        image = fold[p] + fold_in[p, 1] - vec_t[...]
        if p == 0:
            m1 = lanes_to_row(vec_t[...] * image)
            m2 = lanes_to_row(image * image)
            vec_t[...] = image
            vector = two_parts(image)
        images.append(image)
        for group in moves + passed + [legs, legs_b]:
            for copy in group:
                started.append(copy)
    for copy in plane_copies:
        copy.wait_recv()
    summed = tile_b[0]
    for q in range(1, n_lines * n_samp):
        summed = summed + tile_b[q]
    m0 = summed[0:1, 0:traits]
    m1 = summed[1:2, 0:traits]
    m2 = summed[2:3, 0:traits]
    m3 = summed[3:4, 0:traits] - m2
    tau = penalty[...] + 1.0
    mu1 = tau * m0 + m1
    alpha0 = m0 / mu1
    g = m1 / mu1
    rr1 = alpha0 * alpha0 * m2 - g * g * m0
    beta0 = rr1 / m0
    inner = g * g * m1 - 2.0 * g * alpha0 * m2 + alpha0 * alpha0 * m3
    curve = tau * rr1 + inner - beta0 * rr1 / alpha0
    alpha1 = rr1 / curve
    lead = g + beta0
    b = marg[...]
    p1, p2 = images
    factors[...] = jnp.zeros_like(factors)
    factors[0:1, 0:traits] = alpha0 + alpha1 * lead
    factors[1:2, 0:traits] = alpha1 * alpha0
    factors[2:3, 0:traits] = g - alpha1 * lead * tau
    factors[3:4, 0:traits] = alpha1 * (alpha0 * tau - lead) - alpha0
    columns = factors[...].T
    e_b, cross_term, r_b, r_p1 = (columns[:traits, q : q + 1] for q in range(4))
    effects[...] = e_b * b - cross_term * p1
    residual[...] = r_b * b + r_p1 * p1 + cross_term * p2
    for copy in started + stat_copies + width_copies + line_copies + plane_copies:
        copy.wait_send()


def solution(mesh):
    n_samp, n_snp = mesh.shape["samp"], mesh.shape["snp"]
    line = min(LINE, n_snp // 2)

    def step(dosage, band_width, marginal, penalty):
        mine, block = dosage.shape
        traits = marginal.shape[1]
        chunk = mine // CHUNKS
        seats = n_samp * n_snp // line
        dma = pltpu.SemaphoreType.DMA
        f32, bf16 = jnp.float32, jnp.bfloat16
        anywhere = pl.BlockSpec(memory_space=pl.ANY)
        vmem = pl.BlockSpec(memory_space=pltpu.VMEM)
        shape = jax.ShapeDtypeStruct((traits, block), f32)
        effects, residual = pl.pallas_call(
            functools.partial(kernel, n_samp, n_snp, line, mine * n_samp),
            out_shape=(shape, shape),
            in_specs=[anywhere, pl.BlockSpec(memory_space=pltpu.SMEM), anywhere, vmem],
            out_specs=(vmem, vmem),
            scratch_shapes=[
                pltpu.VMEM((CHUNKS, chunk, block), bf16),
                pltpu.VMEM((traits, block), f32),
                pltpu.VMEM((n_samp, 2, block), f32),
                pltpu.VMEM((4, 8, 128), f32),
                pltpu.VMEM((traits, block), f32),
                pltpu.VMEM((2, CHUNKS, traits, chunk), bf16),
                pltpu.VMEM((CHUNKS, traits, chunk), f32),
                pltpu.VMEM((2, 6, CHUNKS, traits, chunk), bf16),
                pltpu.VMEM((2, traits, block), f32),
                pltpu.VMEM((2, traits, block), f32),
                pltpu.VMEM((2, 2, traits, block), f32),
                pltpu.VMEM((line, 8, 128), f32),
                pltpu.VMEM((seats, 8, 128), f32),
                pltpu.VMEM((8, 128), f32),
                dma((CHUNKS,)),
                dma,
                dma((n_samp - 1,)), dma((n_samp - 1,)),
                dma((3,)), dma((3,)),
                dma((2, 6, CHUNKS)), dma((2, 6, CHUNKS)),
                dma((2, 2, 2)), dma((2, 2, 2)),
                dma((line - 1,)), dma((line - 1,)),
                dma((seats - 1,)), dma((seats - 1,)),
            ],
            compiler_params=pltpu.CompilerParams(
                collective_id=0, has_side_effects=True,
                vmem_limit_bytes=60 * 1024 * 1024,
            ),
        )(dosage, band_width, marginal.T, penalty[None, :])
        return effects.T, residual.T

    in_specs = (P("samp", "snp"), P("snp"), P("snp", None), P())
    out_specs = (P("snp", None), P("snp", None))
    return jax.shard_map(step, mesh=mesh, in_specs=in_specs, out_specs=out_specs, check_vma=False)
```

```python
import functools

import jax
import jax.numpy as jnp
from jax import lax
from jax.experimental import pallas as pl
from jax.experimental.pallas import tpu as pltpu
from jax.sharding import PartitionSpec as P

MESH = pl.DeviceIdType.MESH
CHUNKS = 4
LINE = 16
GRANT = 56203674
REACH = (2, 3, 6)


def two_parts(x):
    high = x.astype(jnp.bfloat16)
    low = (x - high.astype(jnp.float32)).astype(jnp.bfloat16)
    return jnp.concatenate([high, low], 0)


def lanes_to_row(x):
    width = x.shape[1]
    total = x[:, 0:128]
    for start in range(128, width, 128):
        total = total + x[:, start : start + 128]
    return jnp.sum(total.T, axis=0, keepdims=True)


def kernel(
    n_samp, n_snp, line, samples,
    dosage, width_hbm, marginal,
    first_image, second_image, coefs,
    grid, marg, stats, widths, vec_t, own, own_f32, near, part, fold, fold_in,
    tile_a, tile_b, width, width_sem,
    load_sem, marg_sem, stat_send, stat_recv, width_send, width_recv,
    u_send, u_recv, fold_send, fold_recv, a_send, a_recv, b_send, b_recv,
):
    chunk = grid.shape[1]
    block = grid.shape[2]
    traits = vec_t.shape[0]
    half = traits // 2
    y = lax.axis_index("samp")
    i = lax.axis_index("snp")
    core = lax.rem(i, 2)
    side = 2 * core - 1

    def snp_at(step):
        return lax.rem(i + step + n_snp, n_snp)

    def samp_at(step):
        return lax.rem(y + step, n_samp)

    loads = []
    for k in range(CHUNKS):
        copy = pltpu.make_async_copy(
            dosage.at[pl.ds(k * chunk, chunk), :], grid.at[k], load_sem.at[k]
        )
        copy.start()
        loads.append(copy)
    marg_copy = pltpu.make_async_copy(marginal, marg, marg_sem)
    marg_copy.start()
    width_copy = pltpu.make_async_copy(width_hbm, width, width_sem)
    width_copy.start()

    spot = lax.rem(i, line)
    base = i - spot
    line_peers = [(y, base + lax.rem(spot + d, line)) for d in range(1, line)]
    n_lines = n_snp // line
    plane_peers = []
    for dx in range(n_lines):
        for dy in range(n_samp):
            if dx or dy:
                plane_peers.append((samp_at(dy), lax.rem(i + line * dx, n_snp)))
    near_peers = [(y, snp_at(d)) for d in (-3, -2, -1, 1, 2, 3)]
    barrier = pltpu.get_barrier_semaphore()
    y_peers = [(samp_at(d), i) for d in range(1, n_samp)]
    x_peers = [(y, lax.rem(i + line * d, n_snp)) for d in range(1, n_lines)]
    far_steps = [d for d in REACH if 2 * d <= line]
    far_peers = [
        (y, base + lax.rem(spot + e, line)) for d in far_steps for e in (d, line - d)
    ]
    everyone = near_peers + y_peers + x_peers + far_peers
    for peer in everyone:
        pl.semaphore_signal(barrier, inc=1, device_id=peer, device_id_type=MESH)

    def send(src, dst, send_sem, recv_sem, peer):
        return pltpu.make_async_remote_copy(
            src_ref=src, dst_ref=dst, send_sem=send_sem, recv_sem=recv_sem,
            device_id=peer, device_id_type=MESH,
        )

    width_copy.wait()
    own_width = width[0].astype(jnp.float32)
    widths[0] = jnp.full(widths.shape[1:], own_width, jnp.float32)
    rows = 64
    sums = (jnp.zeros((8, block), jnp.float32), jnp.zeros((8, block), jnp.float32))
    for k in range(CHUNKS):
        loads[k].wait()

        def add_rows(r, carry, k=k):
            first, second = carry
            g = grid[k, pl.ds(pl.multiple_of(r * rows, rows), rows), :].astype(jnp.float32)
            g = g.reshape(rows // 8, 8, block)
            return first + jnp.sum(g, 0), second + jnp.sum(g * g, 0)

        sums = lax.fori_loop(0, chunk // rows, add_rows, sums)
    stats[0, 0:1, :] = jnp.sum(sums[0], 0, keepdims=True)
    stats[0, 1:2, :] = jnp.sum(sums[1], 0, keepdims=True)

    pl.semaphore_wait(barrier, len(everyone))

    started = []
    stat_copies = []
    for d in range(1, n_samp):
        copy = send(
            stats.at[0], stats.at[d], stat_send.at[d - 1], stat_recv.at[d - 1],
            (samp_at(d), i),
        )
        copy.start()
        stat_copies.append(copy)
    width_copies = []
    for d in (1, 2, 3):
        copy = send(
            widths.at[0], widths.at[d], width_send.at[d - 1], width_recv.at[d - 1],
            (y, snp_at(d)),
        )
        copy.start()
        width_copies.append(copy)

    marg_copy.wait()
    vec_t[...] = marg[...]
    m0 = lanes_to_row(marg[...] * marg[...])
    vector = two_parts(marg[...])

    for copy in stat_copies:
        copy.wait_recv()
    first = (stats[0] + stats[2]) + (stats[1] + stats[3])
    center = first[0:1, :] / samples
    spread = first[1:2, :] / samples - center * center
    scale = lax.rsqrt(spread + 1e-05)

    partner = (y, snp_at(-side))
    forth = (y, snp_at(2 * side))
    back = (y, snp_at(-2 * side))
    outer = (y, snp_at(side))

    masks = {}

    def make_masks():
        for copy in width_copies:
            copy.wait_recv()
        right = {}
        left = {}
        for d in (1, 2, 3):
            allowed = jnp.where(widths[0][0:1, 0:1] >= d, 1.0, 0.0)
            inside = jnp.where(i + d < n_snp, 1.0, 0.0)
            right[d] = allowed * inside
            allowed = jnp.where(widths[d][0:1, 0:1] >= d, 1.0, 0.0)
            inside = jnp.where(i - d >= 0, 1.0, 0.0)
            left[d] = allowed * inside
        turn = jnp.where(core == 1, 1.0, 0.0)
        for d in (1, 2, 3):
            masks["in", d] = turn * left[d] + (1.0 - turn) * right[d]
            masks["out", d] = turn * right[d] + (1.0 - turn) * left[d]

    order = ((0, ("in", 1)), (1, ("in", 2)), (2, ("in", 3)),
             (3, ("out", 1)), (4, ("out", 2)), (5, ("out", 3)))

    def fold_copy(p, leg, piece, peer):
        cut = pl.ds(piece * half, half)
        source = part.at[p] if leg == 0 else fold.at[p]
        return send(
            source.at[cut], fold_in.at[p, leg, cut],
            fold_send.at[p, leg, piece], fold_recv.at[p, leg, piece], peer,
        )

    flipped = y + 1 - 2 * lax.rem(y, 2)
    mirrored = n_samp - 1 - y
    images = []
    trail = None
    cross = []
    for p in range(2):
        moves = []
        for k in range(CHUNKS):
            if p == 0:
                def standardize(r, carry, k=k):
                    cut = pl.ds(pl.multiple_of(r * rows, rows), rows)
                    g = grid[k, cut, :].astype(jnp.float32)
                    grid[k, cut, :] = ((g - center) * scale).astype(jnp.bfloat16)
                    return carry

                lax.fori_loop(0, chunk // rows, standardize, 0)
            u = lax.dot_general(
                vector, grid[k], (((1,), (1,)), ((), ())),
                preferred_element_type=jnp.float32,
            )
            u = u[:traits] + u[traits:]
            own_f32[k] = u
            own[p, k] = u.astype(jnp.bfloat16)
            here = []
            for leg, (slot, peer) in enumerate(((1, forth), (4, back), (0, partner))):
                copy = send(
                    own.at[p, k], near.at[p, slot, k],
                    u_send.at[p, slot, k], u_recv.at[p, slot, k], peer,
                )
                copy.start()
                here.append(copy)
            moves.append(here)
        if p == 0:
            make_masks()
        else:
            m1 = lanes_to_row(marg[...] * images[0])
            m2 = lanes_to_row(images[0] * images[0])
        passed = []
        for k in range(CHUNKS):
            inward, outward, beside = moves[k]
            inward.wait_recv()
            relay = send(
                near.at[p, 1, k], near.at[p, 5, k],
                u_send.at[p, 5, k], u_recv.at[p, 5, k], outer,
            )
            relay.start()
            to_one = send(
                near.at[p, 1, k], near.at[p, 3, k],
                u_send.at[p, 3, k], u_recv.at[p, 3, k], partner,
            )
            to_one.start()
            outward.wait_recv()
            to_three = send(
                near.at[p, 4, k], near.at[p, 2, k],
                u_send.at[p, 2, k], u_recv.at[p, 2, k], partner,
            )
            to_three.start()
            passed.append((to_one, to_three, relay))
        total = jnp.zeros((2 * traits, block), jnp.float32)
        for k in range(CHUNKS):
            moves[k][2].wait_recv()
            for copy in passed[k]:
                copy.wait_recv()
            u = own_f32[k]
            w = u
            for slot, key in order:
                w = w + masks[key] * near[p, slot, k].astype(jnp.float32)
            if p == 1:
                piece = u * w
                folded = piece[:, 0:128]
                for start in range(128, chunk, 128):
                    folded = folded + piece[:, start : start + 128]
                cross.append(folded)
            if p == 1 and k == CHUNKS - 1:
                m3 = lanes_to_row(sum(cross[1:], cross[0])) * (1.0 / samples)
                tile_a[spot] = jnp.zeros(tile_a.shape[1:], jnp.float32)
                share = 1.0 / n_samp
                tile_a[spot, 0:1, 0:traits] = m0 * share
                tile_a[spot, 1:2, 0:traits] = m1 * share
                tile_a[spot, 2:3, 0:traits] = m2 * share
                tile_a[spot, 3:4, 0:traits] = m3
                line_copies = []
                for d, peer in enumerate(line_peers):
                    copy = send(
                        tile_a.at[spot], tile_a.at[spot], a_send.at[d], a_recv.at[d], peer
                    )
                    copy.start()
                    line_copies.append(copy)
            total = total + lax.dot_general(
                two_parts(w), grid[k], (((1,), (0,)), ((), ())),
                preferred_element_type=jnp.float32,
            )
        part[p] = (total[:traits] + total[traits:]) * (1.0 / samples)
        legs = [fold_copy(p, 0, 0, (flipped, i)), fold_copy(p, 0, 1, (mirrored, i))]
        for copy in legs:
            copy.start()
        for copy in legs:
            copy.wait_recv()
        fold[p] = part[p] + fold_in[p, 0]
        legs_b = [fold_copy(p, 1, 0, (mirrored, i)), fold_copy(p, 1, 1, (flipped, i))]
        for copy in legs_b:
            copy.start()
        if p == 1:
            for copy in line_copies:
                copy.wait_recv()
            summed = tile_a[0]
            for q in range(1, line):
                summed = summed + tile_a[q]
            seat = (i // line) * n_samp + y
            tile_b[seat] = summed
            plane_copies = []
            for d, peer in enumerate(plane_peers):
                copy = send(
                    tile_b.at[seat], tile_b.at[seat], b_send.at[d], b_recv.at[d], peer
                )
                copy.start()
                plane_copies.append(copy)
        for copy in legs_b:
            copy.wait_recv()
        image = fold[p] + fold_in[p, 1] - vec_t[...]
        if p == 0:
            vector = two_parts(image)
            vec_t[...] = image
        images.append(image)
        for group in moves + passed + [legs, legs_b]:
            for copy in group:
                started.append(copy)
    for copy in plane_copies:
        copy.wait_recv()
    summed = tile_b[0]
    for q in range(1, n_lines * n_samp):
        summed = summed + tile_b[q]
    coefs[...] = summed
    p1, p2 = images
    first_image[...] = p1
    second_image[...] = p2
    for copy in started + stat_copies + width_copies + line_copies + plane_copies:
        copy.wait_send()


def solution(mesh):
    n_samp, n_snp = mesh.shape["samp"], mesh.shape["snp"]
    line = min(LINE, n_snp // 2)

    def step(dosage, band_width, marginal, penalty):
        mine, block = dosage.shape
        traits = marginal.shape[1]
        chunk = mine // CHUNKS
        seats = n_samp * n_snp // line
        dma = pltpu.SemaphoreType.DMA
        f32, bf16 = jnp.float32, jnp.bfloat16
        anywhere = pl.BlockSpec(memory_space=pl.ANY)
        vmem = pl.BlockSpec(memory_space=pltpu.VMEM)
        shape = jax.ShapeDtypeStruct((traits, block), f32)
        p1, p2, coefs = pl.pallas_call(
            functools.partial(kernel, n_samp, n_snp, line, mine * n_samp),
            out_shape=(shape, shape, jax.ShapeDtypeStruct((8, 128), f32)),
            in_specs=[anywhere, anywhere, anywhere],
            out_specs=(vmem, vmem, vmem),
            scratch_shapes=[
                pltpu.VMEM((CHUNKS, chunk, block), bf16),
                pltpu.VMEM((traits, block), f32),
                pltpu.VMEM((n_samp, 2, block), f32),
                pltpu.VMEM((4, 8, 128), f32),
                pltpu.VMEM((traits, block), f32),
                pltpu.VMEM((2, CHUNKS, traits, chunk), bf16),
                pltpu.VMEM((CHUNKS, traits, chunk), f32),
                pltpu.VMEM((2, 6, CHUNKS, traits, chunk), bf16),
                pltpu.VMEM((2, traits, block), f32),
                pltpu.VMEM((2, traits, block), f32),
                pltpu.VMEM((2, 2, traits, block), f32),
                pltpu.VMEM((line, 8, 128), f32),
                pltpu.VMEM((seats, 8, 128), f32),
                pltpu.SMEM((1,), jnp.int32),
                dma,
                dma((CHUNKS,)),
                dma,
                dma((n_samp - 1,)), dma((n_samp - 1,)),
                dma((3,)), dma((3,)),
                dma((2, 6, CHUNKS)), dma((2, 6, CHUNKS)),
                dma((2, 2, 2)), dma((2, 2, 2)),
                dma((line - 1,)), dma((line - 1,)),
                dma((seats - 1,)), dma((seats - 1,)),
            ],
            compiler_params=pltpu.CompilerParams(
                collective_id=0, has_side_effects=True,
                vmem_limit_bytes=GRANT,
            ),
        )(dosage, band_width, marginal.T)
        m0, m1, m2, mixed = (coefs[q, :traits] for q in range(4))
        m3 = mixed - m2
        tau = penalty + 1.0
        mu1 = tau * m0 + m1
        alpha0 = m0 / mu1
        g = m1 / mu1
        rr1 = alpha0 * alpha0 * m2 - g * g * m0
        beta0 = rr1 / m0
        inner = g * g * m1 - 2.0 * g * alpha0 * m2 + alpha0 * alpha0 * m3
        curve = tau * rr1 + inner - beta0 * rr1 / alpha0
        alpha1 = rr1 / curve
        lead = g + beta0
        cross = alpha1 * alpha0
        b = marginal.T
        effects = (alpha0 + alpha1 * lead)[:, None] * b - cross[:, None] * p1
        residual = (
            (g - alpha1 * lead * tau)[:, None] * b
            + (cross * tau - alpha1 * lead - alpha0)[:, None] * p1
            + cross[:, None] * p2
        )
        return effects.T, residual.T

    in_specs = (P("samp", "snp"), P("snp"), P("snp", None), P())
    out_specs = (P("snp", None), P("snp", None))
    return jax.shard_map(step, mesh=mesh, in_specs=in_specs, out_specs=out_specs, check_vma=False)
```

```python
import functools

import jax
import jax.numpy as jnp
from jax import lax
from jax.experimental import pallas as pl
from jax.experimental.pallas import tpu as pltpu
from jax.sharding import PartitionSpec as P

MESH = pl.DeviceIdType.MESH
CHUNKS = 1
LINE = 16
PARTS = 2
TAIL = 128
GRANT = 56203674
REACH = (2, 3, 6)


def two_parts(x):
    high = x.astype(jnp.bfloat16)
    low = (x - high.astype(jnp.float32)).astype(jnp.bfloat16)
    return jnp.concatenate([high, low], 0)


def lanes_to_row(x):
    width = x.shape[1]
    total = x[:, 0:128]
    for start in range(128, width, 128):
        total = total + x[:, start : start + 128]
    return jnp.sum(total.T, axis=0, keepdims=True)


def kernel(
    n_samp, n_snp, line, samples,
    dosage, width_hbm, marginal,
    first_image, second_image, coefs,
    grid, marg, stats, widths, own, own_f32, near, part, fold, fold_in,
    tile_a, tile_b, width, width_sem,
    load_sem, marg_sem, stat_send, stat_recv, width_send, width_recv,
    u_send, u_recv, fold_send, fold_recv, a_send, a_recv, b_send, b_recv,
):
    chunk = grid.shape[1]
    block = grid.shape[2]
    traits = marg.shape[0]
    half = own.shape[3]
    y = lax.axis_index("samp")
    i = lax.axis_index("snp")
    core = lax.rem(i, 2)
    side = 2 * core - 1

    def snp_at(step):
        return lax.rem(i + step + n_snp, n_snp)

    def samp_at(step):
        return lax.rem(y + step, n_samp)

    loads = []
    for k in range(CHUNKS):
        copy = pltpu.make_async_copy(
            dosage.at[pl.ds(k * chunk, chunk), :], grid.at[k], load_sem.at[k]
        )
        copy.start()
        loads.append(copy)
    marg_copy = pltpu.make_async_copy(marginal, marg, marg_sem)
    marg_copy.start()
    width_copy = pltpu.make_async_copy(width_hbm, width, width_sem)
    width_copy.start()

    spot = lax.rem(i, line)
    base = i - spot
    line_peers = [(y, base + lax.rem(spot + d, line)) for d in range(1, line)]
    n_lines = n_snp // line
    plane_peers = []
    for dx in range(n_lines):
        for dy in range(n_samp):
            if dx or dy:
                plane_peers.append((samp_at(dy), lax.rem(i + line * dx, n_snp)))
    near_peers = [(y, snp_at(d)) for d in (-3, -2, -1, 1, 2, 3)]
    barrier = pltpu.get_barrier_semaphore()
    y_peers = [(samp_at(d), i) for d in range(1, n_samp)]
    x_peers = [(y, lax.rem(i + line * d, n_snp)) for d in range(1, n_lines)]
    far_steps = [d for d in REACH if 2 * d <= line]
    far_peers = [
        (y, base + lax.rem(spot + e, line)) for d in far_steps for e in (d, line - d)
    ]
    everyone = near_peers + y_peers + x_peers + far_peers
    for peer in everyone:
        pl.semaphore_signal(barrier, inc=1, device_id=peer, device_id_type=MESH)

    def send(src, dst, send_sem, recv_sem, peer):
        return pltpu.make_async_remote_copy(
            src_ref=src, dst_ref=dst, send_sem=send_sem, recv_sem=recv_sem,
            device_id=peer, device_id_type=MESH,
        )

    width_copy.wait()
    own_width = width[0].astype(jnp.float32)
    widths[0] = jnp.full(widths.shape[1:], own_width, jnp.float32)
    rows = 64
    sums = (jnp.zeros((8, block), jnp.float32), jnp.zeros((8, block), jnp.float32))
    for k in range(CHUNKS):
        loads[k].wait()

        def add_rows(r, carry, k=k):
            first, second = carry
            g = grid[k, pl.ds(pl.multiple_of(r * rows, rows), rows), :].astype(jnp.float32)
            g = g.reshape(rows // 8, 8, block)
            return first + jnp.sum(g, 0), second + jnp.sum(g * g, 0)

        sums = lax.fori_loop(0, chunk // rows, add_rows, sums)
    stats[0, 0:1, :] = jnp.sum(sums[0], 0, keepdims=True)
    stats[0, 1:2, :] = jnp.sum(sums[1], 0, keepdims=True)

    pl.semaphore_wait(barrier, len(everyone))

    started = []
    stat_copies = []
    for d in range(1, n_samp):
        copy = send(
            stats.at[0], stats.at[d], stat_send.at[d - 1], stat_recv.at[d - 1],
            (samp_at(d), i),
        )
        copy.start()
        stat_copies.append(copy)
    width_copies = []
    for d in (1, 2, 3):
        copy = send(
            widths.at[0], widths.at[d], width_send.at[d - 1], width_recv.at[d - 1],
            (y, snp_at(d)),
        )
        copy.start()
        width_copies.append(copy)

    marg_copy.wait()
    m0 = lanes_to_row(marg[...] * marg[...])
    vector = two_parts(marg[...])

    for copy in stat_copies:
        copy.wait_recv()
    first = (stats[0] + stats[2]) + (stats[1] + stats[3])
    center = first[0:1, :] / samples
    spread = first[1:2, :] / samples - center * center
    scale = lax.rsqrt(spread + 1e-05)

    partner = (y, snp_at(-side))
    forth = (y, snp_at(2 * side))
    back = (y, snp_at(-2 * side))
    outer = (y, snp_at(side))

    masks = {}

    def make_masks():
        for copy in width_copies:
            copy.wait_recv()
        right = {}
        left = {}
        for d in (1, 2, 3):
            allowed = jnp.where(widths[0][0:1, 0:1] >= d, 1.0, 0.0)
            inside = jnp.where(i + d < n_snp, 1.0, 0.0)
            right[d] = allowed * inside
            allowed = jnp.where(widths[d][0:1, 0:1] >= d, 1.0, 0.0)
            inside = jnp.where(i - d >= 0, 1.0, 0.0)
            left[d] = allowed * inside
        turn = jnp.where(core == 1, 1.0, 0.0)
        for d in (1, 2, 3):
            masks["in", d] = turn * left[d] + (1.0 - turn) * right[d]
            masks["out", d] = turn * right[d] + (1.0 - turn) * left[d]

    order = ((0, ("in", 1)), (1, ("in", 2)), (2, ("in", 3)),
             (3, ("out", 1)), (4, ("out", 2)), (5, ("out", 3)))

    def fold_copy(p, h, leg, piece, peer):
        cut = pl.ds(piece * (half // 2), half // 2)
        source = part.at[p, h] if leg == 0 else fold.at[p, h]
        return send(
            source.at[cut], fold_in.at[p, leg, h, cut],
            fold_send.at[p, leg, h, piece], fold_recv.at[p, leg, h, piece], peer,
        )

    flipped = (y + 1 - 2 * lax.rem(y, 2), i)
    mirrored = (n_samp - 1 - y, i)
    halves = range(traits // half)
    moves, passed, legs = {}, {}, {}
    cross = {}

    def hop(p, h, k, source, slot, peer):
        copy = send(
            source, near.at[p, h, slot, k],
            u_send.at[p, h, slot, k], u_recv.at[p, h, slot, k], peer,
        )
        copy.start()
        return copy

    def send_own(p, h, k):
        moves[p, h, k] = [
            hop(p, h, k, own.at[p, h, k], slot, peer)
            for slot, peer in ((1, forth), (4, back), (0, partner))
        ]

    def project(vector, k):
        u = lax.dot_general(
            vector, grid[k], (((1,), (1,)), ((), ())),
            preferred_element_type=jnp.float32,
        )
        rows_out = vector.shape[0] // 2
        return u[:rows_out] + u[rows_out:]

    def keep(p, h, k, u):
        own_f32[h, k] = u
        peak = jnp.maximum(jnp.max(jnp.abs(u), 1, keepdims=True), 1e-30)
        power = jnp.ceil(jnp.log2(peak * (1.0 / 32000.0)))
        coded = jnp.round(u * jnp.exp2(-power))
        own[p, h, k, :, 0:chunk] = coded.astype(jnp.int32).astype(jnp.int16)
        tail = jnp.broadcast_to(power, (u.shape[0], TAIL))
        own[p, h, k, :, chunk:] = tail.astype(jnp.int32).astype(jnp.int16)

    def forward(p, h):
        for k in range(CHUNKS):
            inward, outward, _ = moves[p, h, k]
            inward.wait_recv()
            relay = hop(p, h, k, near.at[p, h, 1, k], 5, outer)
            to_one = hop(p, h, k, near.at[p, h, 1, k], 3, partner)
            outward.wait_recv()
            to_three = hop(p, h, k, near.at[p, h, 4, k], 2, partner)
            passed[p, h, k] = [to_one, to_three, relay]

    def banded(p, h, k):
        moves[p, h, k][2].wait_recv()
        for copy in passed[p, h, k]:
            copy.wait_recv()
        u = own_f32[h, k]
        w = u
        for slot, key in order:
            coded = near[p, h, slot, k, :, 0:chunk].astype(jnp.int32).astype(jnp.float32)
            power = near[p, h, slot, k, :, chunk:].astype(jnp.int32).astype(jnp.float32)
            w = w + (masks[key] * jnp.exp2(power[:, 0:1])) * coded
        if p == 1:
            piece = u * w
            folded = piece[:, 0:128]
            for start in range(128, chunk, 128):
                folded = folded + piece[:, start : start + 128]
            cross[h] = cross[h] + folded if k else folded
        return two_parts(w)

    def gather_back(w, k):
        return lax.dot_general(
            w, grid[k], (((1,), (0,)), ((), ())), preferred_element_type=jnp.float32
        )

    def apply_band(p, h, before_last):
        total = None
        for k in range(CHUNKS):
            w = banded(p, h, k)
            if k == CHUNKS - 1:
                before_last()
            term = gather_back(w, k)
            total = term if total is None else total + term
        part[p, h] = (total[:half] + total[half:]) * (1.0 / samples)
        legs[p, h, 0] = [fold_copy(p, h, 0, 0, flipped), fold_copy(p, h, 0, 1, mirrored)]
        for copy in legs[p, h, 0]:
            copy.start()

    def fold_once(p, h):
        for copy in legs[p, h, 0]:
            copy.wait_recv()
        fold[p, h] = part[p, h] + fold_in[p, 0, h]
        legs[p, h, 1] = [fold_copy(p, h, 1, 0, mirrored), fold_copy(p, h, 1, 1, flipped)]
        for copy in legs[p, h, 1]:
            copy.start()

    def fold_twice(p, h):
        for copy in legs[p, h, 1]:
            copy.wait_recv()
        return fold[p, h] + fold_in[p, 1, h]

    def trait_cut(h):
        return pl.ds(h * half, half)

    for k in range(CHUNKS):
        def standardize(r, carry, k=k):
            cut = pl.ds(pl.multiple_of(r * rows, rows), rows)
            g = grid[k, cut, :].astype(jnp.float32)
            grid[k, cut, :] = ((g - center) * scale).astype(jnp.bfloat16)
            return carry

        lax.fori_loop(0, chunk // rows, standardize, 0)
        u = project(vector, k)
        for h in halves:
            keep(0, h, k, u[h * half : (h + 1) * half])
        send_own(0, 0, k)
    for h in halves[1:]:
        for k in range(CHUNKS):
            send_own(0, h, k)
    make_masks()
    for h in halves:
        forward(0, h)
    for h in halves:
        apply_band(0, h, lambda: None)
    for h in halves:
        fold_once(0, h)

    for h in halves:
        image = fold_twice(0, h) - marg[trait_cut(h), :]
        first_image[trait_cut(h), :] = image
        vector = two_parts(image)
        for k in range(CHUNKS):
            keep(1, h, k, project(vector, k))
            send_own(1, h, k)
    m1 = lanes_to_row(marg[...] * first_image[...])
    m2 = lanes_to_row(first_image[...] * first_image[...])
    line_copies = []

    def send_sums():
        share = 1.0 / n_samp
        m3 = lanes_to_row(jnp.concatenate([cross[h] for h in halves], 0))
        tile_a[spot, 0:1, :] = jnp.concatenate([m0 * share, m1 * share], 1)
        tile_a[spot, 1:2, :] = jnp.concatenate([m2 * share, m3 * (1.0 / samples)], 1)
        for d, peer in enumerate(line_peers):
            copy = send(
                tile_a.at[spot], tile_a.at[spot], a_send.at[d], a_recv.at[d], peer
            )
            copy.start()
            line_copies.append(copy)

    for h in halves:
        forward(1, h)
    for h in halves:
        apply_band(1, h, send_sums if h == halves[-1] else lambda: None)
    for h in halves:
        fold_once(1, h)
    for copy in line_copies:
        copy.wait_recv()
    summed = tile_a[0]
    for q in range(1, line):
        summed = summed + tile_a[q]
    seat = (i // line) * n_samp + y
    tile_b[seat] = summed
    plane_copies = []
    for d, peer in enumerate(plane_peers):
        copy = send(
            tile_b.at[seat], tile_b.at[seat], b_send.at[d], b_recv.at[d], peer
        )
        copy.start()
        plane_copies.append(copy)
    for h in halves:
        second_image[trait_cut(h), :] = fold_twice(1, h) - first_image[trait_cut(h), :]
    for table in (moves, passed, legs):
        for group in table.values():
            started.extend(group)
    for copy in plane_copies:
        copy.wait_recv()
    summed = tile_b[0]
    for q in range(1, n_lines * n_samp):
        summed = summed + tile_b[q]
    coefs[...] = summed
    for copy in started + stat_copies + width_copies + line_copies + plane_copies:
        copy.wait_send()


def solution(mesh):
    n_samp, n_snp = mesh.shape["samp"], mesh.shape["snp"]
    line = min(LINE, n_snp // 2)

    def step(dosage, band_width, marginal, penalty):
        mine, block = dosage.shape
        traits = marginal.shape[1]
        chunk = mine // CHUNKS
        parts, half = PARTS, traits // PARTS
        seats = n_samp * n_snp // line
        dma = pltpu.SemaphoreType.DMA
        f32, bf16 = jnp.float32, jnp.bfloat16
        anywhere = pl.BlockSpec(memory_space=pl.ANY)
        vmem = pl.BlockSpec(memory_space=pltpu.VMEM)
        shape = jax.ShapeDtypeStruct((traits, block), f32)
        p1, p2, coefs = pl.pallas_call(
            functools.partial(kernel, n_samp, n_snp, line, mine * n_samp),
            out_shape=(shape, shape, jax.ShapeDtypeStruct((2, 128), f32)),
            in_specs=[anywhere, anywhere, anywhere],
            out_specs=(vmem, vmem, vmem),
            scratch_shapes=[
                pltpu.VMEM((CHUNKS, chunk, block), bf16),
                pltpu.VMEM((traits, block), f32),
                pltpu.VMEM((n_samp, 2, block), f32),
                pltpu.VMEM((4, 8, 128), f32),
                pltpu.VMEM((2, parts, CHUNKS, half, chunk + TAIL), jnp.int16),
                pltpu.VMEM((parts, CHUNKS, half, chunk), f32),
                pltpu.VMEM((2, parts, 6, CHUNKS, half, chunk + TAIL), jnp.int16),
                pltpu.VMEM((2, parts, half, block), f32),
                pltpu.VMEM((2, parts, half, block), f32),
                pltpu.VMEM((2, 2, parts, half, block), f32),
                pltpu.VMEM((line, 2, 128), f32),
                pltpu.VMEM((seats, 2, 128), f32),
                pltpu.SMEM((1,), jnp.int32),
                dma,
                dma((CHUNKS,)),
                dma,
                dma((n_samp - 1,)), dma((n_samp - 1,)),
                dma((3,)), dma((3,)),
                dma((2, parts, 6, CHUNKS)), dma((2, parts, 6, CHUNKS)),
                dma((2, 2, parts, 2)), dma((2, 2, parts, 2)),
                dma((line - 1,)), dma((line - 1,)),
                dma((seats - 1,)), dma((seats - 1,)),
            ],
            compiler_params=pltpu.CompilerParams(
                collective_id=0, has_side_effects=True,
                vmem_limit_bytes=GRANT,
            ),
        )(dosage, band_width, marginal.T)
        m0, m1, m2, mixed = (
            coefs[q // 2, q % 2 * traits : (q % 2 + 1) * traits] for q in range(4)
        )
        m3 = mixed - m2
        tau = penalty + 1.0
        mu1 = tau * m0 + m1
        alpha0 = m0 / mu1
        g = m1 / mu1
        rr1 = alpha0 * alpha0 * m2 - g * g * m0
        beta0 = rr1 / m0
        inner = g * g * m1 - 2.0 * g * alpha0 * m2 + alpha0 * alpha0 * m3
        curve = tau * rr1 + inner - beta0 * rr1 / alpha0
        alpha1 = rr1 / curve
        lead = g + beta0
        cross = alpha1 * alpha0
        b = marginal.T
        effects = (alpha0 + alpha1 * lead)[:, None] * b - cross[:, None] * p1
        residual = (
            (g - alpha1 * lead * tau)[:, None] * b
            + (cross * tau - alpha1 * lead - alpha0)[:, None] * p1
            + cross[:, None] * p2
        )
        return effects.T, residual.T

    in_specs = (P("samp", "snp"), P("snp"), P("snp", None), P())
    out_specs = (P("snp", None), P("snp", None))
    return jax.shard_map(step, mesh=mesh, in_specs=in_specs, out_specs=out_specs, check_vma=False)
```

```python
import functools

import jax
import jax.numpy as jnp
from jax import lax
from jax.experimental import pallas as pl
from jax.experimental.pallas import tpu as pltpu
from jax.sharding import PartitionSpec as P

MESH = pl.DeviceIdType.MESH
CHUNKS = 1
LINE = 16
PARTS = 2
TAIL = 128
GRANT = 56203674
REACH = (2, 3, 6)


def two_parts(x):
    high = x.astype(jnp.bfloat16)
    low = (x - high.astype(jnp.float32)).astype(jnp.bfloat16)
    return jnp.concatenate([high, low], 0)


def lanes_to_row(x):
    width = x.shape[1]
    total = x[:, 0:128]
    for start in range(128, width, 128):
        total = total + x[:, start : start + 128]
    return jnp.sum(total.T, axis=0, keepdims=True)


def kernel(
    n_samp, n_snp, line, samples,
    dosage, width_hbm, marginal,
    first_image, second_image, coefs,
    grid, marg, stats, widths, own, own_f32, near, brief, brief_in, part, fold, fold_in,
    tile_a, tile_b, width, width_sem,
    load_sem, marg_sem, stat_send, stat_recv, width_send, width_recv,
    u_send, u_recv, brief_send, brief_recv, fold_send, fold_recv, a_send, a_recv, b_send, b_recv,
):
    chunk = grid.shape[1]
    block = grid.shape[2]
    traits = marg.shape[0]
    half = own.shape[3]
    y = lax.axis_index("samp")
    i = lax.axis_index("snp")
    core = lax.rem(i, 2)
    side = 2 * core - 1

    def snp_at(step):
        return lax.rem(i + step + n_snp, n_snp)

    def samp_at(step):
        return lax.rem(y + step, n_samp)

    loads = []
    for k in range(CHUNKS):
        copy = pltpu.make_async_copy(
            dosage.at[pl.ds(k * chunk, chunk), :], grid.at[k], load_sem.at[k]
        )
        copy.start()
        loads.append(copy)
    marg_copy = pltpu.make_async_copy(marginal, marg, marg_sem)
    marg_copy.start()
    width_copy = pltpu.make_async_copy(width_hbm, width, width_sem)
    width_copy.start()

    spot = lax.rem(i, line)
    base = i - spot
    line_peers = [(y, base + lax.rem(spot + d, line)) for d in range(1, line)]
    n_lines = n_snp // line
    plane_peers = []
    for dx in range(n_lines):
        for dy in range(n_samp):
            if dx or dy:
                plane_peers.append((samp_at(dy), lax.rem(i + line * dx, n_snp)))
    near_peers = [(y, snp_at(d)) for d in (-3, -2, -1, 1, 2, 3)]
    barrier = pltpu.get_barrier_semaphore()
    y_peers = [(samp_at(d), i) for d in range(1, n_samp)]
    x_peers = [(y, lax.rem(i + line * d, n_snp)) for d in range(1, n_lines)]
    far_steps = [d for d in REACH if 2 * d <= line]
    far_peers = [
        (y, base + lax.rem(spot + e, line)) for d in far_steps for e in (d, line - d)
    ]
    everyone = near_peers + y_peers + x_peers + far_peers
    for peer in everyone:
        pl.semaphore_signal(barrier, inc=1, device_id=peer, device_id_type=MESH)

    def send(src, dst, send_sem, recv_sem, peer):
        return pltpu.make_async_remote_copy(
            src_ref=src, dst_ref=dst, send_sem=send_sem, recv_sem=recv_sem,
            device_id=peer, device_id_type=MESH,
        )

    width_copy.wait()
    own_width = width[0].astype(jnp.float32)
    widths[0] = jnp.full(widths.shape[1:], own_width, jnp.float32)
    rows = 64
    sums = (jnp.zeros((8, block), jnp.float32), jnp.zeros((8, block), jnp.float32))
    for k in range(CHUNKS):
        loads[k].wait()

        def add_rows(r, carry, k=k):
            first, second = carry
            g = grid[k, pl.ds(pl.multiple_of(r * rows, rows), rows), :].astype(jnp.float32)
            g = g.reshape(rows // 8, 8, block)
            return first + jnp.sum(g, 0), second + jnp.sum(g * g, 0)

        sums = lax.fori_loop(0, chunk // rows, add_rows, sums)
    stats[0, 0:1, :] = jnp.sum(sums[0], 0, keepdims=True)
    stats[0, 1:2, :] = jnp.sum(sums[1], 0, keepdims=True)

    pl.semaphore_wait(barrier, len(everyone))

    started = []
    stat_copies = []
    for d in range(1, n_samp):
        copy = send(
            stats.at[0], stats.at[d], stat_send.at[d - 1], stat_recv.at[d - 1],
            (samp_at(d), i),
        )
        copy.start()
        stat_copies.append(copy)
    width_copies = []
    for d in (1, 2, 3):
        copy = send(
            widths.at[0], widths.at[d], width_send.at[d - 1], width_recv.at[d - 1],
            (y, snp_at(d)),
        )
        copy.start()
        width_copies.append(copy)

    marg_copy.wait()
    m0 = lanes_to_row(marg[...] * marg[...])
    vector = two_parts(marg[...])

    for copy in stat_copies:
        copy.wait_recv()
    first = (stats[0] + stats[2]) + (stats[1] + stats[3])
    center = first[0:1, :] / samples
    spread = first[1:2, :] / samples - center * center
    scale = lax.rsqrt(spread + 1e-05)

    partner = (y, snp_at(-side))
    forth = (y, snp_at(2 * side))
    back = (y, snp_at(-2 * side))
    outer = (y, snp_at(side))

    masks = {}

    def make_masks():
        for copy in width_copies:
            copy.wait_recv()
        right = {}
        left = {}
        for d in (1, 2, 3):
            allowed = jnp.where(widths[0][0:1, 0:1] >= d, 1.0, 0.0)
            inside = jnp.where(i + d < n_snp, 1.0, 0.0)
            right[d] = allowed * inside
            allowed = jnp.where(widths[d][0:1, 0:1] >= d, 1.0, 0.0)
            inside = jnp.where(i - d >= 0, 1.0, 0.0)
            left[d] = allowed * inside
        turn = jnp.where(core == 1, 1.0, 0.0)
        for d in (1, 2, 3):
            masks["in", d] = turn * left[d] + (1.0 - turn) * right[d]
            masks["out", d] = turn * right[d] + (1.0 - turn) * left[d]

    order = ((0, ("in", 1)), (1, ("in", 2)), (2, ("in", 3)),
             (3, ("out", 1)), (4, ("out", 2)), (5, ("out", 3)))

    def fold_copy(p, h, leg, piece, peer):
        cut = pl.ds(piece * (half // 2), half // 2)
        source = part.at[p, h] if leg == 0 else fold.at[p, h]
        return send(
            source.at[cut], fold_in.at[p, leg, h, cut],
            fold_send.at[p, leg, h, piece], fold_recv.at[p, leg, h, piece], peer,
        )

    flipped = (y + 1 - 2 * lax.rem(y, 2), i)
    mirrored = (n_samp - 1 - y, i)
    halves = range(traits // half)
    moves, passed, legs, briefs = {}, {}, {}, {}
    cross = {}

    def hop(p, h, k, source, slot, peer):
        copy = send(
            source, near.at[p, h, slot, k],
            u_send.at[p, h, slot, k], u_recv.at[p, h, slot, k], peer,
        )
        copy.start()
        return copy

    def send_own(p, h, k):
        moves[p, h, k] = [
            hop(p, h, k, own.at[p, h, k], slot, peer)
            for slot, peer in ((1, forth), (4, back), (0, partner))
        ]

    def project(vector, k):
        u = lax.dot_general(
            vector, grid[k], (((1,), (1,)), ((), ())),
            preferred_element_type=jnp.float32,
        )
        rows_out = vector.shape[0] // 2
        return u[:rows_out] + u[rows_out:]

    def pack(target, values):
        wide = values.shape[1]
        peak = jnp.maximum(jnp.max(jnp.abs(values), 1, keepdims=True), 1e-30)
        power = jnp.ceil(jnp.log2(peak * (1.0 / 32000.0)))
        coded = jnp.round(values * jnp.exp2(-power))
        target[:, 0:wide] = coded.astype(jnp.int32).astype(jnp.int16)
        tail = jnp.broadcast_to(power, (values.shape[0], TAIL))
        target[:, wide:] = tail.astype(jnp.int32).astype(jnp.int16)

    def unpack(source, factor):
        wide = source.shape[1] - TAIL
        coded = source[:, 0:wide].astype(jnp.int32).astype(jnp.float32)
        power = source[:, wide:].astype(jnp.int32).astype(jnp.float32)
        return (factor * jnp.exp2(power[:, 0:1])) * coded

    def keep(p, h, k, u):
        own_f32[h, k] = u
        pack(own.at[p, h, k], u)

    def forward(p, h):
        for k in range(CHUNKS):
            inward, outward, _ = moves[p, h, k]
            inward.wait_recv()
            relay = hop(p, h, k, near.at[p, h, 1, k], 5, outer)
            to_one = hop(p, h, k, near.at[p, h, 1, k], 3, partner)
            outward.wait_recv()
            to_three = hop(p, h, k, near.at[p, h, 4, k], 2, partner)
            passed[p, h, k] = [to_one, to_three, relay]

    def banded(p, h, k):
        moves[p, h, k][2].wait_recv()
        for copy in passed[p, h, k]:
            copy.wait_recv()
        u = own_f32[h, k]
        w = u
        for slot, key in order:
            w = w + unpack(near.at[p, h, slot, k], masks[key])
        if p == 1:
            piece = u * w
            folded = piece[:, 0:128]
            for start in range(128, chunk, 128):
                folded = folded + piece[:, start : start + 128]
            cross[h] = cross[h] + folded if k else folded
        return two_parts(w)

    def gather_back(w, k):
        return lax.dot_general(
            w, grid[k], (((1,), (0,)), ((), ())), preferred_element_type=jnp.float32
        )

    def apply_band(p, h, before_last):
        total = None
        for k in range(CHUNKS):
            w = banded(p, h, k)
            if k == CHUNKS - 1:
                before_last()
            term = gather_back(w, k)
            total = term if total is None else total + term
        part[p, h] = (total[:half] + total[half:]) * (1.0 / samples)
        if p == 1:
            fold_start(p, h)
            return
        pack(brief.at[h], part[p, h])
        briefs[h] = []
        for d in range(1, n_samp):
            copy = send(
                brief.at[h], brief_in.at[h, d - 1],
                brief_send.at[h, d - 1], brief_recv.at[h, d - 1], (samp_at(d), i),
            )
            copy.start()
            briefs[h].append(copy)

    def fold_start(p, h):
        legs[p, h, 0] = [fold_copy(p, h, 0, 0, flipped), fold_copy(p, h, 0, 1, mirrored)]
        for copy in legs[p, h, 0]:
            copy.start()

    def fold_once(p, h):
        for copy in legs[p, h, 0]:
            copy.wait_recv()
        fold[p, h] = part[p, h] + fold_in[p, 0, h]
        legs[p, h, 1] = [fold_copy(p, h, 1, 0, mirrored), fold_copy(p, h, 1, 1, flipped)]
        for copy in legs[p, h, 1]:
            copy.start()

    def fold_twice(p, h):
        for copy in legs[p, h, 1]:
            copy.wait_recv()
        return fold[p, h] + fold_in[p, 1, h]

    def trait_cut(h):
        return pl.ds(h * half, half)

    strip = min(256, chunk)
    for k in range(CHUNKS):
        for first_row in range(0, chunk, strip):
            cut = pl.ds(first_row, strip)
            g = grid[k, cut, :].astype(jnp.float32)
            scaled = ((g - center) * scale).astype(jnp.bfloat16)
            grid[k, cut, :] = scaled
            u = lax.dot_general(
                vector, scaled, (((1,), (1,)), ((), ())),
                preferred_element_type=jnp.float32,
            )
            u = u[:traits] + u[traits:]
            for h in halves:
                own_f32[h, k, :, cut] = u[h * half : (h + 1) * half]
        pack(own.at[0, 0, k], own_f32[0, k])
        send_own(0, 0, k)
    for h in halves[1:]:
        for k in range(CHUNKS):
            pack(own.at[0, h, k], own_f32[h, k])
            send_own(0, h, k)
    make_masks()
    for h in halves:
        forward(0, h)
    for h in halves:
        apply_band(0, h, lambda: None)
    for h in halves:
        rough = part[0, h] - marg[trait_cut(h), :]
        for d, copy in enumerate(briefs[h]):
            copy.wait_recv()
            rough = rough + unpack(brief_in.at[h, d], 1.0)
        vector = two_parts(rough)
        for k in range(CHUNKS):
            keep(1, h, k, project(vector, k))
            send_own(1, h, k)
    line_copies = []

    def send_sums():
        share = 1.0 / n_samp
        m3 = lanes_to_row(jnp.concatenate([cross[h] for h in halves], 0))
        tile_a[spot, 0:1, :] = jnp.concatenate([m0 * share, m1 * share], 1)
        tile_a[spot, 1:2, :] = jnp.concatenate([m2 * share, m3 * (1.0 / samples)], 1)
        for d, peer in enumerate(line_peers):
            copy = send(
                tile_a.at[spot], tile_a.at[spot], a_send.at[d], a_recv.at[d], peer
            )
            copy.start()
            line_copies.append(copy)

    for h in halves:
        fold_start(0, h)
    for h in halves:
        forward(1, h)
        if h == 0:
            for other in halves:
                fold_once(0, other)
    for h in halves:
        first_image[trait_cut(h), :] = fold_twice(0, h) - marg[trait_cut(h), :]
    m1 = lanes_to_row(marg[...] * first_image[...])
    m2 = lanes_to_row(first_image[...] * first_image[...])
    for h in halves:
        apply_band(1, h, send_sums if h == halves[-1] else lambda: None)
    for h in halves:
        fold_once(1, h)
    for copy in line_copies:
        copy.wait_recv()
    summed = tile_a[0]
    for q in range(1, line):
        summed = summed + tile_a[q]
    seat = (i // line) * n_samp + y
    tile_b[seat] = summed
    plane_copies = []
    for d, peer in enumerate(plane_peers):
        copy = send(
            tile_b.at[seat], tile_b.at[seat], b_send.at[d], b_recv.at[d], peer
        )
        copy.start()
        plane_copies.append(copy)
    for h in halves:
        second_image[trait_cut(h), :] = fold_twice(1, h) - first_image[trait_cut(h), :]
    for table in (moves, passed, legs, briefs):
        for group in table.values():
            started.extend(group)
    for copy in plane_copies:
        copy.wait_recv()
    summed = tile_b[0]
    for q in range(1, n_lines * n_samp):
        summed = summed + tile_b[q]
    coefs[...] = summed
    for copy in started + stat_copies + width_copies + line_copies + plane_copies:
        copy.wait_send()


def solution(mesh):
    n_samp, n_snp = mesh.shape["samp"], mesh.shape["snp"]
    line = min(LINE, n_snp // 2)

    def step(dosage, band_width, marginal, penalty):
        mine, block = dosage.shape
        traits = marginal.shape[1]
        chunk = mine // CHUNKS
        parts, half = PARTS, traits // PARTS
        seats = n_samp * n_snp // line
        dma = pltpu.SemaphoreType.DMA
        f32, bf16 = jnp.float32, jnp.bfloat16
        anywhere = pl.BlockSpec(memory_space=pl.ANY)
        vmem = pl.BlockSpec(memory_space=pltpu.VMEM)
        shape = jax.ShapeDtypeStruct((traits, block), f32)
        p1, p2, coefs = pl.pallas_call(
            functools.partial(kernel, n_samp, n_snp, line, mine * n_samp),
            out_shape=(shape, shape, jax.ShapeDtypeStruct((2, 128), f32)),
            in_specs=[anywhere, anywhere, anywhere],
            out_specs=(vmem, vmem, vmem),
            scratch_shapes=[
                pltpu.VMEM((CHUNKS, chunk, block), bf16),
                pltpu.VMEM((traits, block), f32),
                pltpu.VMEM((n_samp, 2, block), f32),
                pltpu.VMEM((4, 8, 128), f32),
                pltpu.VMEM((2, parts, CHUNKS, half, chunk + TAIL), jnp.int16),
                pltpu.VMEM((parts, CHUNKS, half, chunk), f32),
                pltpu.VMEM((2, parts, 6, CHUNKS, half, chunk + TAIL), jnp.int16),
                pltpu.VMEM((parts, half, block + TAIL), jnp.int16),
                pltpu.VMEM((parts, n_samp - 1, half, block + TAIL), jnp.int16),
                pltpu.VMEM((2, parts, half, block), f32),
                pltpu.VMEM((2, parts, half, block), f32),
                pltpu.VMEM((2, 2, parts, half, block), f32),
                pltpu.VMEM((line, 2, 128), f32),
                pltpu.VMEM((seats, 2, 128), f32),
                pltpu.SMEM((1,), jnp.int32),
                dma,
                dma((CHUNKS,)),
                dma,
                dma((n_samp - 1,)), dma((n_samp - 1,)),
                dma((3,)), dma((3,)),
                dma((2, parts, 6, CHUNKS)), dma((2, parts, 6, CHUNKS)),
                dma((parts, n_samp - 1)), dma((parts, n_samp - 1)),
                dma((2, 2, parts, 2)), dma((2, 2, parts, 2)),
                dma((line - 1,)), dma((line - 1,)),
                dma((seats - 1,)), dma((seats - 1,)),
            ],
            compiler_params=pltpu.CompilerParams(
                collective_id=0, has_side_effects=True,
                vmem_limit_bytes=GRANT,
            ),
        )(dosage, band_width, marginal.T)
        m0, m1, m2, mixed = (
            coefs[q // 2, q % 2 * traits : (q % 2 + 1) * traits] for q in range(4)
        )
        m3 = mixed - m2
        tau = penalty + 1.0
        mu1 = tau * m0 + m1
        inverse = 1.0 / mu1
        alpha0 = m0 * inverse
        g = m1 * inverse
        beta0 = (m0 * m2 - m1 * m1) * inverse * inverse
        rr1 = m0 * beta0
        inner = g * g * m1 - 2.0 * g * alpha0 * m2 + alpha0 * alpha0 * m3
        curve = tau * rr1 + inner - beta0 * beta0 * mu1
        alpha1 = rr1 / curve
        lead = g + beta0
        cross = alpha1 * alpha0
        b = marginal.T
        effects = (alpha0 + alpha1 * lead)[:, None] * b - cross[:, None] * p1
        residual = (
            (g - alpha1 * lead * tau)[:, None] * b
            + (cross * tau - alpha1 * lead - alpha0)[:, None] * p1
            + cross[:, None] * p2
        )
        return effects.T, residual.T

    in_specs = (P("samp", "snp"), P("snp"), P("snp", None), P())
    out_specs = (P("snp", None), P("snp", None))
    return jax.shard_map(step, mesh=mesh, in_specs=in_specs, out_specs=out_specs, check_vma=False)
```

```python
import functools

import jax
import jax.numpy as jnp
from jax import lax
from jax.experimental import pallas as pl
from jax.experimental.pallas import tpu as pltpu
from jax.sharding import PartitionSpec as P

MESH = pl.DeviceIdType.MESH
CHUNKS = 1
LINE = 16
PARTS = 2
TAIL = 128
GRANT = 56203674
REACH = (2, 3, 6)


def two_parts(x):
    high = x.astype(jnp.bfloat16)
    low = (x - high.astype(jnp.float32)).astype(jnp.bfloat16)
    return jnp.concatenate([high, low], 0)


def lanes_to_row(x):
    width = x.shape[1]
    total = x[:, 0:128]
    for start in range(128, width, 128):
        total = total + x[:, start : start + 128]
    return jnp.sum(total.T, axis=0, keepdims=True)


def kernel(
    n_samp, n_snp, line, samples,
    dosage, width_hbm, marginal,
    first_image, second_image, coefs,
    grid, marg, stats, widths, own, own_f32, near, brief, brief_in, part, fold, fold_in,
    tile_a, tile_b, width, width_sem,
    load_sem, marg_sem, stat_send, stat_recv, width_send, width_recv,
    u_send, u_recv, brief_send, brief_recv, fold_send, fold_recv, a_send, a_recv, b_send, b_recv,
):
    chunk = grid.shape[1]
    block = grid.shape[2]
    traits = marg.shape[0]
    half = own.shape[3]
    y = lax.axis_index("samp")
    i = lax.axis_index("snp")
    core = lax.rem(i, 2)
    side = 2 * core - 1

    def snp_at(step):
        return lax.rem(i + step + n_snp, n_snp)

    def samp_at(step):
        return lax.rem(y + step, n_samp)

    loads = []
    for k in range(CHUNKS):
        copy = pltpu.make_async_copy(
            dosage.at[pl.ds(k * chunk, chunk), :], grid.at[k], load_sem.at[k]
        )
        copy.start()
        loads.append(copy)
    marg_copy = pltpu.make_async_copy(marginal, marg, marg_sem)
    marg_copy.start()
    width_copy = pltpu.make_async_copy(width_hbm, width, width_sem)
    width_copy.start()

    spot = lax.rem(i, line)
    base = i - spot
    line_peers = [(y, base + lax.rem(spot + d, line)) for d in range(1, line)]
    n_lines = n_snp // line
    plane_peers = []
    for dx in range(n_lines):
        for dy in range(n_samp):
            if dx or dy:
                plane_peers.append((samp_at(dy), lax.rem(i + line * dx, n_snp)))
    near_peers = [(y, snp_at(d)) for d in (-3, -2, -1, 1, 2, 3)]
    barrier = pltpu.get_barrier_semaphore()
    y_peers = [(samp_at(d), i) for d in range(1, n_samp)]
    x_peers = [(y, lax.rem(i + line * d, n_snp)) for d in range(1, n_lines)]
    far_steps = [d for d in REACH if 2 * d <= line]
    far_peers = [
        (y, base + lax.rem(spot + e, line)) for d in far_steps for e in (d, line - d)
    ]
    everyone = near_peers + y_peers + x_peers + far_peers
    for peer in everyone:
        pl.semaphore_signal(barrier, inc=1, device_id=peer, device_id_type=MESH)

    def send(src, dst, send_sem, recv_sem, peer):
        return pltpu.make_async_remote_copy(
            src_ref=src, dst_ref=dst, send_sem=send_sem, recv_sem=recv_sem,
            device_id=peer, device_id_type=MESH,
        )

    width_copy.wait()
    own_width = width[0].astype(jnp.float32)
    widths[0] = jnp.full(widths.shape[1:], own_width, jnp.float32)
    rows = 64
    sums = (jnp.zeros((8, block), jnp.float32), jnp.zeros((8, block), jnp.float32))
    for k in range(CHUNKS):
        loads[k].wait()

        def add_rows(r, carry, k=k):
            first, second = carry
            g = grid[k, pl.ds(pl.multiple_of(r * rows, rows), rows), :].astype(jnp.float32)
            g = g.reshape(rows // 8, 8, block)
            return first + jnp.sum(g, 0), second + jnp.sum(g * g, 0)

        sums = lax.fori_loop(0, chunk // rows, add_rows, sums)
    stats[0, 0:1, :] = jnp.sum(sums[0], 0, keepdims=True)
    stats[0, 1:2, :] = jnp.sum(sums[1], 0, keepdims=True)

    pl.semaphore_wait(barrier, len(everyone))

    started = []
    stat_copies = []
    for d in range(1, n_samp):
        copy = send(
            stats.at[0], stats.at[d], stat_send.at[d - 1], stat_recv.at[d - 1],
            (samp_at(d), i),
        )
        copy.start()
        stat_copies.append(copy)
    width_copies = []
    for d in (1, 2, 3):
        copy = send(
            widths.at[0], widths.at[d], width_send.at[d - 1], width_recv.at[d - 1],
            (y, snp_at(d)),
        )
        copy.start()
        width_copies.append(copy)

    marg_copy.wait()
    m0 = lanes_to_row(marg[...] * marg[...])
    vector = two_parts(marg[...])

    for copy in stat_copies:
        copy.wait_recv()
    first = (stats[0] + stats[2]) + (stats[1] + stats[3])
    center = first[0:1, :] / samples
    spread = first[1:2, :] / samples - center * center
    scale = lax.rsqrt(spread + 1e-05)

    partner = (y, snp_at(-side))
    forth = (y, snp_at(2 * side))
    back = (y, snp_at(-2 * side))
    outer = (y, snp_at(side))

    masks = {}

    def make_masks():
        for copy in width_copies:
            copy.wait_recv()
        right = {}
        left = {}
        for d in (1, 2, 3):
            allowed = jnp.where(widths[0][0:1, 0:1] >= d, 1.0, 0.0)
            inside = jnp.where(i + d < n_snp, 1.0, 0.0)
            right[d] = allowed * inside
            allowed = jnp.where(widths[d][0:1, 0:1] >= d, 1.0, 0.0)
            inside = jnp.where(i - d >= 0, 1.0, 0.0)
            left[d] = allowed * inside
        turn = jnp.where(core == 1, 1.0, 0.0)
        for d in (1, 2, 3):
            masks["in", d] = turn * left[d] + (1.0 - turn) * right[d]
            masks["out", d] = turn * right[d] + (1.0 - turn) * left[d]

    order = ((0, ("in", 1)), (1, ("in", 2)), (2, ("in", 3)),
             (3, ("out", 1)), (4, ("out", 2)), (5, ("out", 3)))

    def fold_copy(p, h, leg, piece, peer):
        cut = pl.ds(piece * (half // 2), half // 2)
        source = part.at[p, h] if leg == 0 else fold.at[p, h]
        return send(
            source.at[cut], fold_in.at[p, leg, h, cut],
            fold_send.at[p, leg, h, piece], fold_recv.at[p, leg, h, piece], peer,
        )

    flipped = (y + 1 - 2 * lax.rem(y, 2), i)
    mirrored = (n_samp - 1 - y, i)
    halves = range(traits // half)
    moves, passed, legs, briefs = {}, {}, {}, {}
    cross = {}

    def hop(p, h, k, source, slot, peer):
        copy = send(
            source, near.at[p, h, slot, k],
            u_send.at[p, h, slot, k], u_recv.at[p, h, slot, k], peer,
        )
        copy.start()
        return copy

    def send_own(p, h, k):
        moves[p, h, k] = [
            hop(p, h, k, own.at[p, h, k], slot, peer)
            for slot, peer in ((1, forth), (4, back), (0, partner))
        ]

    def project(vector, k):
        u = lax.dot_general(
            vector, grid[k], (((1,), (1,)), ((), ())),
            preferred_element_type=jnp.float32,
        )
        rows_out = vector.shape[0] // 2
        return u[:rows_out] + u[rows_out:]

    def pack(target, values):
        wide = values.shape[1]
        peak = jnp.maximum(jnp.max(jnp.abs(values), 1, keepdims=True), 1e-30)
        power = jnp.ceil(jnp.log2(peak * (1.0 / 32000.0)))
        coded = jnp.round(values * jnp.exp2(-power))
        target[:, 0:wide] = coded.astype(jnp.int32).astype(jnp.int16)
        tail = jnp.broadcast_to(power, (values.shape[0], TAIL))
        target[:, wide:] = tail.astype(jnp.int32).astype(jnp.int16)

    def unpack(source, factor):
        wide = source.shape[1] - TAIL
        coded = source[:, 0:wide].astype(jnp.int32).astype(jnp.float32)
        power = source[:, wide:].astype(jnp.int32).astype(jnp.float32)
        return (factor * jnp.exp2(power[:, 0:1])) * coded

    def keep(p, h, k, u):
        own_f32[h, k] = u
        pack(own.at[p, h, k], u)

    def forward(p, h):
        for k in range(CHUNKS):
            inward, outward, _ = moves[p, h, k]
            inward.wait_recv()
            relay = hop(p, h, k, near.at[p, h, 1, k], 5, outer)
            to_one = hop(p, h, k, near.at[p, h, 1, k], 3, partner)
            outward.wait_recv()
            to_three = hop(p, h, k, near.at[p, h, 4, k], 2, partner)
            passed[p, h, k] = [to_one, to_three, relay]

    def banded(p, h, k):
        to_one, to_three, relay = passed[p, h, k]
        arrivals = {0: moves[p, h, k][2], 3: to_one, 2: to_three, 5: relay}
        u = own_f32[h, k]
        w = u
        keys = dict(order)
        for slot in (0, 1, 4, 3, 2, 5):
            if slot in arrivals:
                arrivals[slot].wait_recv()
            w = w + unpack(near.at[p, h, slot, k], masks[keys[slot]])
        if p == 1:
            piece = u * w
            folded = piece[:, 0:128]
            for start in range(128, chunk, 128):
                folded = folded + piece[:, start : start + 128]
            cross[h] = cross[h] + folded if k else folded
        return two_parts(w)

    def gather_back(w, k):
        return lax.dot_general(
            w, grid[k], (((1,), (0,)), ((), ())), preferred_element_type=jnp.float32
        )

    def apply_band(p, h, before_last):
        total = None
        for k in range(CHUNKS):
            w = banded(p, h, k)
            if k == CHUNKS - 1:
                before_last()
            term = gather_back(w, k)
            total = term if total is None else total + term
        part[p, h] = (total[:half] + total[half:]) * (1.0 / samples)
        if p == 1:
            fold_start(p, h)
            return
        pack(brief.at[h], part[p, h])
        briefs[h] = []
        for d in range(1, n_samp):
            copy = send(
                brief.at[h], brief_in.at[h, d - 1],
                brief_send.at[h, d - 1], brief_recv.at[h, d - 1], (samp_at(d), i),
            )
            copy.start()
            briefs[h].append(copy)

    def fold_start(p, h):
        legs[p, h, 0] = [fold_copy(p, h, 0, 0, flipped), fold_copy(p, h, 0, 1, mirrored)]
        for copy in legs[p, h, 0]:
            copy.start()

    def fold_once(p, h):
        for copy in legs[p, h, 0]:
            copy.wait_recv()
        fold[p, h] = part[p, h] + fold_in[p, 0, h]
        legs[p, h, 1] = [fold_copy(p, h, 1, 0, mirrored), fold_copy(p, h, 1, 1, flipped)]
        for copy in legs[p, h, 1]:
            copy.start()

    def fold_twice(p, h):
        for copy in legs[p, h, 1]:
            copy.wait_recv()
        return fold[p, h] + fold_in[p, 1, h]

    def trait_cut(h):
        return pl.ds(h * half, half)

    strip = min(256, chunk)
    for k in range(CHUNKS):
        for first_row in range(0, chunk, strip):
            cut = pl.ds(first_row, strip)
            g = grid[k, cut, :].astype(jnp.float32)
            scaled = ((g - center) * scale).astype(jnp.bfloat16)
            grid[k, cut, :] = scaled
            u = lax.dot_general(
                vector, scaled, (((1,), (1,)), ((), ())),
                preferred_element_type=jnp.float32,
            )
            u = u[:traits] + u[traits:]
            for h in halves:
                own_f32[h, k, :, cut] = u[h * half : (h + 1) * half]
        pack(own.at[0, 0, k], own_f32[0, k])
        send_own(0, 0, k)
    for h in halves[1:]:
        for k in range(CHUNKS):
            pack(own.at[0, h, k], own_f32[h, k])
            send_own(0, h, k)
    make_masks()
    for h in halves:
        forward(0, h)
    for h in halves:
        apply_band(0, h, lambda: None)
    for h in halves:
        rough = part[0, h] - marg[trait_cut(h), :]
        for d, copy in enumerate(briefs[h]):
            copy.wait_recv()
            rough = rough + unpack(brief_in.at[h, d], 1.0)
        vector = two_parts(rough)
        for k in range(CHUNKS):
            keep(1, h, k, project(vector, k))
            send_own(1, h, k)
    line_copies = []

    def send_sums():
        share = 1.0 / n_samp
        m3 = lanes_to_row(jnp.concatenate([cross[h] for h in halves], 0))
        tile_a[spot, 0:1, :] = jnp.concatenate([m0 * share, m1 * share], 1)
        tile_a[spot, 1:2, :] = jnp.concatenate([m2 * share, m3 * (1.0 / samples)], 1)
        for d, peer in enumerate(line_peers):
            copy = send(
                tile_a.at[spot], tile_a.at[spot], a_send.at[d], a_recv.at[d], peer
            )
            copy.start()
            line_copies.append(copy)

    for h in halves:
        fold_start(0, h)
    for h in halves:
        forward(1, h)
        if h == 0:
            for other in halves:
                fold_once(0, other)
    for h in halves:
        first_image[trait_cut(h), :] = fold_twice(0, h) - marg[trait_cut(h), :]
    m1 = lanes_to_row(marg[...] * first_image[...])
    m2 = lanes_to_row(first_image[...] * first_image[...])
    for h in halves:
        apply_band(1, h, send_sums if h == halves[-1] else lambda: None)
    for h in halves:
        fold_once(1, h)
    for copy in line_copies:
        copy.wait_recv()
    summed = tile_a[0]
    for q in range(1, line):
        summed = summed + tile_a[q]
    seat = (i // line) * n_samp + y
    tile_b[seat] = summed
    plane_copies = []
    for d, peer in enumerate(plane_peers):
        copy = send(
            tile_b.at[seat], tile_b.at[seat], b_send.at[d], b_recv.at[d], peer
        )
        copy.start()
        plane_copies.append(copy)
    for h in halves:
        second_image[trait_cut(h), :] = fold_twice(1, h) - first_image[trait_cut(h), :]
    for table in (moves, passed, legs, briefs):
        for group in table.values():
            started.extend(group)
    for copy in plane_copies:
        copy.wait_recv()
    summed = tile_b[0]
    for q in range(1, n_lines * n_samp):
        summed = summed + tile_b[q]
    coefs[...] = summed
    for copy in started + stat_copies + width_copies + line_copies + plane_copies:
        copy.wait_send()


def solution(mesh):
    n_samp, n_snp = mesh.shape["samp"], mesh.shape["snp"]
    line = min(LINE, n_snp // 2)

    def step(dosage, band_width, marginal, penalty):
        mine, block = dosage.shape
        traits = marginal.shape[1]
        chunk = mine // CHUNKS
        parts, half = PARTS, traits // PARTS
        seats = n_samp * n_snp // line
        dma = pltpu.SemaphoreType.DMA
        f32, bf16 = jnp.float32, jnp.bfloat16
        anywhere = pl.BlockSpec(memory_space=pl.ANY)
        vmem = pl.BlockSpec(memory_space=pltpu.VMEM)
        shape = jax.ShapeDtypeStruct((traits, block), f32)
        p1, p2, coefs = pl.pallas_call(
            functools.partial(kernel, n_samp, n_snp, line, mine * n_samp),
            out_shape=(shape, shape, jax.ShapeDtypeStruct((2, 128), f32)),
            in_specs=[anywhere, anywhere, anywhere],
            out_specs=(vmem, vmem, vmem),
            scratch_shapes=[
                pltpu.VMEM((CHUNKS, chunk, block), bf16),
                pltpu.VMEM((traits, block), f32),
                pltpu.VMEM((n_samp, 2, block), f32),
                pltpu.VMEM((4, 8, 128), f32),
                pltpu.VMEM((2, parts, CHUNKS, half, chunk + TAIL), jnp.int16),
                pltpu.VMEM((parts, CHUNKS, half, chunk), f32),
                pltpu.VMEM((2, parts, 6, CHUNKS, half, chunk + TAIL), jnp.int16),
                pltpu.VMEM((parts, half, block + TAIL), jnp.int16),
                pltpu.VMEM((parts, n_samp - 1, half, block + TAIL), jnp.int16),
                pltpu.VMEM((2, parts, half, block), f32),
                pltpu.VMEM((2, parts, half, block), f32),
                pltpu.VMEM((2, 2, parts, half, block), f32),
                pltpu.VMEM((line, 2, 128), f32),
                pltpu.VMEM((seats, 2, 128), f32),
                pltpu.SMEM((1,), jnp.int32),
                dma,
                dma((CHUNKS,)),
                dma,
                dma((n_samp - 1,)), dma((n_samp - 1,)),
                dma((3,)), dma((3,)),
                dma((2, parts, 6, CHUNKS)), dma((2, parts, 6, CHUNKS)),
                dma((parts, n_samp - 1)), dma((parts, n_samp - 1)),
                dma((2, 2, parts, 2)), dma((2, 2, parts, 2)),
                dma((line - 1,)), dma((line - 1,)),
                dma((seats - 1,)), dma((seats - 1,)),
            ],
            compiler_params=pltpu.CompilerParams(
                collective_id=0, has_side_effects=True,
                vmem_limit_bytes=GRANT,
            ),
        )(dosage, band_width, marginal.T)
        m0, m1, m2, mixed = (
            coefs[q // 2, q % 2 * traits : (q % 2 + 1) * traits] for q in range(4)
        )
        m3 = mixed - m2
        tau = penalty + 1.0
        mu1 = tau * m0 + m1
        inverse = 1.0 / mu1
        alpha0 = m0 * inverse
        g = m1 * inverse
        beta0 = (m0 * m2 - m1 * m1) * inverse * inverse
        rr1 = m0 * beta0
        inner = g * g * m1 - 2.0 * g * alpha0 * m2 + alpha0 * alpha0 * m3
        curve = tau * rr1 + inner - beta0 * beta0 * mu1
        alpha1 = rr1 / curve
        lead = g + beta0
        cross = alpha1 * alpha0
        b = marginal.T
        effects = (alpha0 + alpha1 * lead)[:, None] * b - cross[:, None] * p1
        residual = (
            (g - alpha1 * lead * tau)[:, None] * b
            + (cross * tau - alpha1 * lead - alpha0)[:, None] * p1
            + cross[:, None] * p2
        )
        return effects.T, residual.T

    in_specs = (P("samp", "snp"), P("snp"), P("snp", None), P())
    out_specs = (P("snp", None), P("snp", None))
    return jax.shard_map(step, mesh=mesh, in_specs=in_specs, out_specs=out_specs, check_vma=False)
```
